512 devices in a mesh: leaf: 512 (over x, z, y, core).
Axes of the slice: x: 4, y: 4, z: 16, core: 2. Of those that a mesh axis runs over, the one named last changes fastest.
Arguments:
- right_sides: bfloat16 [64, 524288], P(None, 'leaf'), may hold values from -6 to 6
- leaf_inverse: bfloat16 [524288, 1024], P('leaf'), may hold values from -0.1875 to 0.1875
- leaf_basis: bfloat16 [524288, 256], P('leaf'), may hold values from -0.1875 to 0.1875
- transfer: bfloat16 [262144, 256], P('leaf'), may hold values from -0.25 to 0.25
- coupling: bfloat16 [262144, 256], P('leaf'), may hold values from -0.25 to 0.25
Outputs:
- solution: bfloat16 [64, 524288], P(None, 'leaf')
The draws below stay inside these ranges and needn't reach their ends.
All inputs are finite; a program needn't handle non-finite values.
Results may differ from the reference program's by a relative error of at most 0.025.
Values may be sent and summed in bfloat16 or wider, within the bound.
No kernel may reach another device: no remote copies, remote signals or barrier semaphores. Data moves between devices by JAX's collectives and lax.ppermute only.
A program may use at most 64 MiB of HBM per device.

```python
import jax
import jax.numpy as jnp
from jax import lax

LEAF = 1024
RANK = 256
COLUMNS = 64
LEVELS = 9
POINTS = 524288
N_LEAF = 512


def shard_levels(stream_key, extent, pieces, low, high):
    def one(axis_at, shards_of):
        heights = jax.random.uniform(jax.random.fold_in(jax.random.fold_in(stream_key, 6), axis_at), (shards_of,), jnp.float32, low / len(pieces), high / len(pieces))
        return jnp.repeat(jnp.exp(heights), extent[axis_at] // shards_of).reshape((-1,) + (1,) * (len(extent) - axis_at - 1))

    loudness = one(*pieces[0])
    for cut in pieces[1:]:
        loudness = loudness * one(*cut)
    return loudness


def noise(rng, dims, scale, reach, shards=(), dtype=jnp.bfloat16):
    level = shard_levels(rng, dims, shards, -0.22, 0.18) if shards else 1.0
    values = jax.random.normal(rng, dims, jnp.float32) * scale * level
    return jnp.minimum(jnp.maximum(values, -reach), reach).astype(dtype)


def setup_inputs(seed: int = 0) -> dict:
    splits = jax.random.split(jax.random.key(seed), 6)
    right_sides = noise(splits[0], (COLUMNS, POINTS), 1.0, 6.0, ((1, 512),))
    leaf_inverse = noise(splits[1], (POINTS, LEAF), LEAF ** -0.5, 0.1875, ((0, 512),))
    leaf_basis = noise(splits[2], (POINTS, RANK), LEAF ** -0.5, 0.1875, ((0, 512),))
    transfer = noise(splits[3], (N_LEAF * 2 * RANK, RANK), (2 * RANK) ** -0.5, 0.25, ((0, 512),))
    coupling = noise(splits[4], (N_LEAF * 2 * RANK, RANK), (2 * RANK) ** -0.5, 0.25, ((0, 512),))
    return dict(right_sides=right_sides, leaf_inverse=leaf_inverse, leaf_basis=leaf_basis, transfer=transfer, coupling=coupling)


def batch_product(left_part, right_part):
    return jnp.einsum("nkr,nrs->nks", left_part.astype(jnp.float32), right_part.astype(jnp.float32), precision=lax.Precision.HIGHEST)


def batch_transposed(left_part, right_part):
    return jnp.einsum("nkr,nsr->nks", left_part.astype(jnp.float32), right_part.astype(jnp.float32), precision=lax.Precision.HIGHEST)


def partner_of(values, distance):
    shaped = values.reshape((-1, 2, distance) + values.shape[1:])
    return shaped[:, ::-1].reshape(values.shape)


def reference(right_sides, leaf_inverse, leaf_basis, transfer, coupling):
    leaves = N_LEAF
    sides = right_sides.reshape(COLUMNS, leaves, LEAF).transpose(1, 0, 2)
    inverses = leaf_inverse.reshape(leaves, LEAF, LEAF)
    bases = leaf_basis.reshape(leaves, LEAF, RANK)
    transfers = transfer.reshape(leaves, 2 * RANK, RANK)
    couplings = coupling.reshape(leaves, 2 * RANK, RANK)
    own_map = transfers[:, :RANK]
    other_map = transfers[:, RANK:]
    from_other = couplings[:, :RANK]
    from_own = couplings[:, RANK:]

    def leaf_skeleton(pair):
        side, basis = pair
        return jnp.dot(side, basis, preferred_element_type=jnp.float32).astype(jnp.bfloat16)

    current = lax.map(leaf_skeleton, (sides, bases))
    own_values = []
    far_values = []
    for tree_level in range(1, LEVELS + 1):
        other = partner_of(current, 2 ** (tree_level - 1))
        own_values.append(current)
        far_values.append(other)
        merged = batch_product(current, own_map) + batch_product(other, other_map)
        current = merged.astype(jnp.bfloat16)
    node_h = current
    for tree_level in range(LEVELS, 0, -1):
        other_h = partner_of(node_h, 2 ** (tree_level - 1))
        total = batch_transposed(node_h, own_map) + batch_transposed(other_h, other_map)
        total = total + batch_product(far_values[tree_level - 1], from_other)
        total = total + batch_product(own_values[tree_level - 1], from_own)
        node_h = total.astype(jnp.bfloat16)

    def leaf_solution(group):
        side, inverse, basis, leaf_h = group
        total = jnp.dot(side, inverse, preferred_element_type=jnp.float32)
        total = total + lax.dot_general(leaf_h, basis, (((1,), (1,)), ((), ())), preferred_element_type=jnp.float32)
        return total.astype(jnp.bfloat16)

    blocks = lax.map(leaf_solution, (sides, inverses, bases, node_h))
    return blocks.transpose(1, 0, 2).reshape(COLUMNS, leaves * LEAF)
```

```python
import jax
import jax.numpy as jnp
from jax import lax
from jax.experimental import pallas as pl
from jax.experimental.pallas import tpu as pltpu
from jax.sharding import PartitionSpec as P


AXIS = "leaf"
BF16 = jnp.bfloat16
F32 = jnp.float32
CHUNKS = 4
VMEM_GRANT = 12 * 2**20


IN_SMEM = pl.BlockSpec(memory_space=pltpu.SMEM)
IN_VMEM = pl.BlockSpec(memory_space=pltpu.VMEM)
IN_HBM = pl.BlockSpec(memory_space=pltpu.HBM)


def swap(block, mask):
    route = [(device, device ^ mask) for device in range(lax.axis_size(AXIS))]
    return lax.ppermute(block, AXIS, route)


def exchange(slots, low, width):
    count, size = lax.axis_size(AXIS), 1 << width
    groups = [
        [base | k << low for k in range(size)]
        for base in range(count)
        if not base & ((size - 1) << low)
    ]
    return lax.all_to_all(slots, AXIS, 0, 0, axis_index_groups=groups)


def times(values, matrix):
    return jnp.dot(values, matrix, preferred_element_type=F32)


def times_t(values, matrix):
    return lax.dot_general(values, matrix, (((1,), (1,)), ((), ())), preferred_element_type=F32)


def product(*matrices):
    total = matrices[0]
    for matrix in matrices[1:]:
        total = times(total, matrix).astype(BF16)
    return total


def call(kernel, outs, ins, specs, scratch=(), grant=VMEM_GRANT):
    outs = [jax.ShapeDtypeStruct(shape, dtype) for shape, dtype in outs]
    return pl.pallas_call(
        kernel,
        out_shape=outs,
        in_specs=specs,
        out_specs=[IN_VMEM] * len(outs),
        scratch_shapes=list(scratch),
        compiler_params=pltpu.CompilerParams(vmem_limit_bytes=grant),
    )(*ins)


def fetched(arrays):
    return [pltpu.VMEM(a.shape, a.dtype) for a in arrays] + [pltpu.SemaphoreType.DMA((len(arrays),))]


def start_copies(pairs, arrived):
    copies = [
        pltpu.make_async_copy(source, target, arrived.at[k])
        for k, (source, target) in enumerate(pairs)
    ]
    for copy in copies:
        copy.start()
    return copies


def chunked(source, held):
    rows = held.shape[0] // CHUNKS
    return [(source.at[pl.ds(k * rows, rows)], held.at[pl.ds(k * rows, rows)]) for k in range(CHUNKS)]


def streamed(sides, held, side_copy, copies):
    rows = held.shape[0] // CHUNKS
    side_copy.wait()
    total = None
    for k in range(CHUNKS):
        copies[k].wait()
        part = times(sides[:, k * rows : (k + 1) * rows], held[k * rows : (k + 1) * rows])
        total = part if total is None else total + part
    return total


def dense_kernel(sides_ref, inverse_ref, out_ref, sides, inverse, sem):
    copies = start_copies([(sides_ref, sides)] + chunked(inverse_ref, inverse), sem)
    out_ref[...] = streamed(sides, inverse, copies[0], copies[1:])


def parts(maps_ref):
    rank = maps_ref.shape[1]
    return [maps_ref[k * rank : (k + 1) * rank] for k in range(maps_ref.shape[0] // rank)]


def open_up_z_kernel(me_ref, part_ref, other_ref, maps_ref, own_ref, slots_ref):
    p, q = parts(maps_ref)[:2]
    own = (part_ref[...] + times(other_ref[...], q)).astype(BF16)
    own_ref[...] = own
    for k in range(4):
        slots_ref[k] = own
    slots_ref[(me_ref[0] >> 3 & 3) ^ 2] = times(own, p).astype(BF16)


def prepare_up_z_kernel(far_ref, own_ref, maps_ref, base_ref, mix_ref, far, sem):
    copies = start_copies([(far_ref, far)], sem)
    p, q = parts(maps_ref)[:2]
    base_ref[...] = times(own_ref[...], product(p, p))
    mix_ref[0] = product(q, p)
    mix_ref[1] = q
    copies[0].wait()
    mix_ref[2] = product(far[...], q)


def close_up_z_kernel(me_ref, got_ref, base_ref, mix_ref, out_ref):
    me = me_ref[0] >> 3 & 3
    total = base_ref[...]
    for k in (1, 2, 3):
        total = total + times(got_ref[me ^ k], mix_ref[k - 1])
    out_ref[...] = total.astype(BF16)


def settle_up_z_kernel(me_ref, got_ref, own_ref, far_ref, maps_ref, out_ref, far, sem):
    copies = start_copies([(far_ref, far)], sem)
    me = me_ref[0] >> 3 & 3
    p, q, c, k = parts(maps_ref)
    own, near = own_ref[...], got_ref[me ^ 1]
    out_ref[0] = (times(near, c) + times(own, k)).astype(BF16)
    middle = (times(own, p) + times(near, q)).astype(BF16)
    copies[0].wait()
    across = (got_ref[me ^ 2].astype(F32) + times(got_ref[me ^ 3], far[...])).astype(BF16)
    out_ref[1] = (times(across, c) + times(middle, k)).astype(BF16)


def open_top_kernel(part_ref, other_ref, maps_ref, own_ref, slots_ref):
    own = (part_ref[...] + times(other_ref[...], parts(maps_ref)[1])).astype(BF16)
    own_ref[...] = own
    for k in range(4):
        slots_ref[k] = own


def eighth_kernel(far_ref, maps_ref, out_ref, far, sem):
    copies = start_copies([(far_ref, far)], sem)
    p, q, c, k = parts(maps_ref)
    copies[0].wait()
    far_p, far_q = parts(far)
    eight, far_eight = {0: p, 1: q}, {2: far_p, 3: far_q}
    nine = {j: product(m, p) for j, m in eight.items()}
    nine |= {j: product(m, q) for j, m in far_eight.items()}
    far_nine = {j: product(m, far_p) for j, m in far_eight.items()}
    far_nine |= {j: product(m, far_q) for j, m in eight.items()}
    for j in range(4):
        total = times_t(nine[j], p) + times_t(far_nine[j], q)
        total = total + (times(eight[j], k) if j in eight else times(far_eight[j], c))
        out_ref[j] = total.astype(BF16)


def prepare_top_kernel(near_ref, eighth_ref, own_ref, maps_ref, base_ref, mix_ref, near, eighth, sem):
    copies = start_copies([(near_ref, near), (eighth_ref, eighth)], sem)
    p, q, c, k = parts(maps_ref)
    for copy in copies:
        copy.wait()
    for j in range(4):
        total = times_t(eighth[j], p) + times_t(near[j ^ 1], q)
        if j < 2:
            total = total + (c if j else k).astype(F32)
        matrix = total.astype(BF16)
        if j:
            mix_ref[j - 1] = matrix
        else:
            base_ref[...] = times(own_ref[...], matrix)


def turn(got_shift, product_of, slot_shift, width):
    def kernel(me_ref, got_ref, base_ref, mix_ref, local_ref, maps_ref, own_ref, slots_ref):
        me = me_ref[0]
        total = base_ref[...]
        for k in (1, 2, 3):
            total = total + product_of(got_ref[(me >> got_shift & 3) ^ k], mix_ref[k - 1])
        node = total.astype(BF16)
        own = times_t(node, parts(maps_ref)[0]) + local_ref[...].astype(F32)
        own = own.astype(BF16)
        own_ref[...] = own
        place, half = me >> slot_shift & (1 << width) - 1, 1 << width - 1
        near = place & half
        for k in range(half):
            slots_ref[near | k] = own
            slots_ref[(near ^ half) | k] = node

    return kernel


def prepare_down_kernel(far_ref, own_ref, local_ref, maps_ref, base_ref, mix_ref, far, sem):
    copies = start_copies([(far_ref, far)], sem)
    p, q = parts(maps_ref)[:2]
    base_ref[...] = times_t(own_ref[...], p) + local_ref[...].astype(F32)
    mix_ref[0] = q
    mix_ref[1] = product(p, q)
    copies[0].wait()
    mix_ref[2] = product(q, far[...])


def prepare_down_y_kernel(*refs):
    (core_ref, y1_ref, cy_ref, dense_ref, own_ref, one_ref, two_ref, maps_ref, basis_ref) = refs[:9]
    base_ref, mix_ref, core, y1, cy, dense, sem = refs[9:]
    copies = start_copies([(core_ref, core), (y1_ref, y1), (cy_ref, cy), (dense_ref, dense)], sem)
    p, q = parts(maps_ref)[:2]
    mix = [product(p, p), None, product(p, q), None]
    for copy in copies:
        copy.wait()
    rank = p.shape[0]
    core_p, core_q, core_two = core[:rank], core[rank : 2 * rank], core[2 * rank :]
    mix[1] = product(q, core_p)
    mix[3] = product(q, core_q)
    node = times_t(own_ref[...], mix[0]) + one_ref[...].astype(F32)
    node = node + times_t(two_ref[...], p) + times_t(core_two, q)
    base_ref[...] = dense[...] + times_t(node.astype(BF16), basis_ref[...])
    for k, far in enumerate((q, core_q, y1[...], cy[...])):
        if k:
            mix_ref[k - 1] = mix[k]
        mix_ref[k + 3] = product(mix[k], far)


def finish_kernel(me_ref, got_ref, base_ref, mix_ref, basis_ref, out_ref):
    me = me_ref[0] & 7
    total = None
    for k in range(1, 8):
        part = times_t(got_ref[me ^ k], mix_ref[k - 1])
        total = part if total is None else total + part
    node = total.astype(BF16)
    out_ref[...] = (base_ref[...] + times_t(node, basis_ref[...])).astype(BF16)


def body(right_sides, leaf_inverse, leaf_basis, transfer, coupling):
    rank = leaf_basis.shape[1]
    columns = right_sides.shape[0]
    block, square = (columns, rank), (rank, rank)
    me = lax.axis_index(AXIS).astype(jnp.int32).reshape(1)
    prefetched, local = {}, {}

    def after(values, late):
        return lax.optimization_barrier((values, late))[0]

    def prefetch(name, value, mask, late):
        value = after(value, late)
        prefetched[name] = swap(value, mask)

    current = times(right_sides, leaf_basis).astype(BF16)
    own_map, other_map = transfer[:rank], transfer[rank:]
    from_other, from_own = coupling[:rank], coupling[rank:]

    def settle(level, far, own, late):
        far, own = after((far, own), late)
        total = times(far, from_other) + times(own, from_own)
        local[level] = lax.optimization_barrier(total.astype(BF16))

    def half_up(current, bit):
        other = swap(current, 1 << bit)
        part = times(current, own_map)
        return part, other

    def up(current, bit):
        part, other = half_up(current, bit)
        above = (part + times(other, other_map)).astype(BF16)
        settle(bit + 1, other, current, above)
        return above

    current = up(current, 0)
    maps = jnp.concatenate(after((transfer, coupling), current), 0)
    prefetch("pre_q_z2", after(transfer, current)[rank:], 16, current)
    current = up(current, 1)
    prefetch("pre_x2", transfer, 256, current)
    below = current
    part, other = half_up(below, 2)

    current, slots = call(
        open_up_z_kernel,
        [(block, BF16), ((4, *block), BF16)],
        [me, part, other, maps],
        [IN_SMEM] + [IN_VMEM] * 3,
    )
    settle(3, other, below, current)
    far = prefetched["pre_x2"]
    (eighth,) = call(
        eighth_kernel,
        [((4, *square), BF16)],
        [far, after(maps, slots)],
        [IN_HBM, IN_VMEM],
        fetched([far]),
    )
    prefetch("pre_x1", eighth, 128, slots)
    got = exchange(slots, 3, 2)
    far = prefetched["pre_q_z2"]
    base, mix = call(
        prepare_up_z_kernel,
        [(block, F32), ((3, *square), BF16)],
        [far, current, maps],
        [IN_HBM] + [IN_VMEM] * 2,
        fetched([far]),
    )
    below = current
    (current,) = call(
        close_up_z_kernel, [(block, BF16)], [me, got, base, mix], [IN_SMEM] + [IN_VMEM] * 3
    )
    (settled,) = call(
        settle_up_z_kernel,
        [((2, *block), BF16)],
        [me, got, after(below, current), far, maps],
        [IN_SMEM, IN_VMEM, IN_VMEM, IN_HBM, IN_VMEM],
        fetched([far]),
    )
    current = up(current, 5)
    below = current
    part, other = half_up(below, 6)

    current, slots = call(
        open_top_kernel, [(block, BF16), ((4, *block), BF16)], [part, other, maps], [IN_VMEM] * 3
    )
    settle(7, other, below, current)
    prefetch("pre_q_z4", after(transfer, slots)[rank:], 32, slots)
    got = exchange(slots, 7, 2)
    near = prefetched["pre_x1"]
    base, mix = call(
        prepare_top_kernel,
        [(block, F32), ((3, *square), BF16)],
        [near, eighth, current, maps],
        [IN_HBM] * 2 + [IN_VMEM] * 2,
        fetched([near, eighth]),
    )
    local[4], local[5] = settled[0], settled[1]

    def turn_down(kernel, got, base, mix, level, width):
        return call(
            kernel,
            [(block, BF16), ((1 << width, *block), BF16)],
            [me, got, base, mix, local[level], maps],
            [IN_SMEM] + [IN_VMEM] * 5,
        )

    def prepare_down(far, own, level):
        return call(
            prepare_down_kernel,
            [(block, F32), ((3, *square), BF16)],
            [far, own, local[level], maps],
            [IN_HBM] + [IN_VMEM] * 3,
            fetched([far]),
        )

    own, slots = turn_down(turn(7, times, 5, 2), got, base, mix, 7, 2)
    neighbour_map = after(transfer, slots)[rank:]
    prefetch("pre_q_y1", neighbour_map, 2, slots)
    prefetch("pre_q_cy", neighbour_map, 3, slots)
    prefetch("pre_q_z1", neighbour_map, 8, slots)
    got = exchange(slots, 5, 2)
    base, mix = prepare_down(prefetched["pre_q_z4"], own, 6)

    own, slots = turn_down(turn(5, times_t, 3, 2), got, base, mix, 5, 2)
    prefetch("pre_core", jnp.concatenate(after((maps[: 2 * rank], local[2]), slots), 0), 1, slots)
    got = exchange(slots, 3, 2)
    base, mix = prepare_down(prefetched["pre_q_z1"], own, 4)

    own, slots = turn_down(turn(3, times_t, 0, 3), got, base, mix, 3, 3)
    got = exchange(slots, 0, 3)
    copied = [right_sides, leaf_inverse]
    (dense,) = call(
        dense_kernel,
        [((columns, leaf_inverse.shape[1]), F32)],
        [after(right_sides, slots), leaf_inverse],
        [IN_HBM] * 2,
        [pltpu.VMEM(a.shape, a.dtype) for a in copied] + [pltpu.SemaphoreType.DMA((CHUNKS + 1,))],
        None,
    )
    near = [prefetched[f"pre_{name}"] for name in ("core", "q_y1", "q_cy")]
    base, mix = call(
        prepare_down_y_kernel,
        [(dense.shape, F32), ((7, *square), BF16)],
        [*near, dense, own, local[1], local[2], maps, leaf_basis],
        [IN_HBM] * 4 + [IN_VMEM] * 5,
        fetched([*near, dense]),
    )
    (out,) = call(
        finish_kernel,
        [(dense.shape, BF16)],
        [me, got, base, mix, leaf_basis],
        [IN_SMEM] + [IN_VMEM] * 4,
    )
    return out


def solution(mesh):
    placed = (P(None, AXIS), P(AXIS, None), P(AXIS, None), P(AXIS, None), P(AXIS, None))
    return jax.shard_map(
        body, mesh=mesh, in_specs=placed, out_specs=P(None, AXIS), check_vma=False
    )
```

```python
import jax
import jax.numpy as jnp
from jax import lax
from jax.experimental import pallas as pl
from jax.experimental.pallas import tpu as pltpu
from jax.sharding import PartitionSpec as P


AXIS = "leaf"
BF16 = jnp.bfloat16
F32 = jnp.float32
CHUNKS = 4
VMEM_GRANT = 12 * 2**20


IN_SMEM = pl.BlockSpec(memory_space=pltpu.SMEM)
IN_VMEM = pl.BlockSpec(memory_space=pltpu.VMEM)
IN_HBM = pl.BlockSpec(memory_space=pltpu.HBM)


def swap(block, mask):
    route = [(device, device ^ mask) for device in range(lax.axis_size(AXIS))]
    return lax.ppermute(block, AXIS, route)


def exchange(slots, low, width):
    count, size = lax.axis_size(AXIS), 1 << width
    groups = [
        [base | k << low for k in range(size)]
        for base in range(count)
        if not base & ((size - 1) << low)
    ]
    return lax.all_to_all(slots, AXIS, 0, 0, axis_index_groups=groups)


def times(values, matrix):
    return jnp.dot(values, matrix, preferred_element_type=F32)


def times_t(values, matrix):
    return lax.dot_general(values, matrix, (((1,), (1,)), ((), ())), preferred_element_type=F32)


def product(*matrices):
    total = matrices[0]
    for matrix in matrices[1:]:
        total = times(total, matrix).astype(BF16)
    return total


def call(kernel, outs, ins, specs, scratch=(), grant=VMEM_GRANT):
    outs = [jax.ShapeDtypeStruct(shape, dtype) for shape, dtype in outs]
    return pl.pallas_call(
        kernel,
        out_shape=outs,
        in_specs=specs,
        out_specs=[IN_VMEM] * len(outs),
        scratch_shapes=list(scratch),
        compiler_params=pltpu.CompilerParams(vmem_limit_bytes=grant),
    )(*ins)


def fetched(arrays):
    return [pltpu.VMEM(a.shape, a.dtype) for a in arrays] + [pltpu.SemaphoreType.DMA((len(arrays),))]


def start_copies(pairs, arrived):
    copies = [
        pltpu.make_async_copy(source, target, arrived.at[k])
        for k, (source, target) in enumerate(pairs)
    ]
    for copy in copies:
        copy.start()
    return copies


def stage_kernel(source_ref, out_ref, sem):
    start_copies([(source_ref, out_ref)], sem)[0].wait()


def dense_kernel(sides_ref, inverse_ref, out_ref, sides, inverse, sem):
    rows = inverse.shape[0] // CHUNKS
    cuts = [pl.ds(k * rows, rows) for k in range(CHUNKS)]
    copies = start_copies(
        [(sides_ref, sides)] + [(inverse_ref.at[cut], inverse.at[cut]) for cut in cuts], sem
    )
    copies[0].wait()
    total = None
    for k in range(CHUNKS):
        copies[k + 1].wait()
        cut = slice(k * rows, (k + 1) * rows)
        part = times(sides[:, cut], inverse[cut])
        total = part if total is None else total + part
    out_ref[...] = total


def parts(maps_ref):
    rank = maps_ref.shape[1]
    return [maps_ref[k * rank : (k + 1) * rank] for k in range(maps_ref.shape[0] // rank)]


def open_up_z_kernel(me_ref, part_ref, other_ref, maps_ref, own_ref, slots_ref):
    p, q = parts(maps_ref)
    own = (part_ref[...] + times(other_ref[...], q)).astype(BF16)
    own_ref[...] = own
    for k in range(4):
        slots_ref[k] = own
    slots_ref[(me_ref[0] >> 3 & 3) ^ 2] = times(own, p).astype(BF16)


def prepare_up_z_kernel(far_ref, own_ref, maps_ref, base_ref, mix_ref, far, sem):
    copies = start_copies([(far_ref, far)], sem)
    p, q = parts(maps_ref)
    base_ref[...] = times(own_ref[...], product(p, p))
    mix_ref[0] = product(q, p)
    mix_ref[1] = q
    copies[0].wait()
    mix_ref[2] = product(parts(far)[1], q)


def close_up_z_kernel(me_ref, got_ref, base_ref, mix_ref, out_ref):
    me = me_ref[0] >> 3 & 3
    total = base_ref[...]
    for k in (1, 2, 3):
        total = total + times(got_ref[me ^ k], mix_ref[k - 1])
    out_ref[...] = total.astype(BF16)


def settle_up_z_kernel(me_ref, got_ref, own_ref, far_ref, maps_ref, links_ref, out_ref, far, sem):
    copies = start_copies([(far_ref, far)], sem)
    me = me_ref[0] >> 3 & 3
    (p, q), (c, k) = parts(maps_ref), parts(links_ref)
    own, near = own_ref[...], got_ref[me ^ 1]
    out_ref[0] = (times(near, c) + times(own, k)).astype(BF16)
    middle = (times(own, p) + times(near, q)).astype(BF16)
    copies[0].wait()
    across = (got_ref[me ^ 2].astype(F32) + times(got_ref[me ^ 3], parts(far)[1])).astype(BF16)
    out_ref[1] = (times(across, c) + times(middle, k)).astype(BF16)


def open_top_kernel(part_ref, other_ref, maps_ref, own_ref, slots_ref):
    own = (part_ref[...] + times(other_ref[...], parts(maps_ref)[1])).astype(BF16)
    own_ref[...] = own
    for k in range(4):
        slots_ref[k] = own


def eighth_kernel(far_ref, maps_ref, links_ref, out_ref, far, sem):
    copies = start_copies([(far_ref, far)], sem)
    (p, q), (c, k) = parts(maps_ref), parts(links_ref)
    copies[0].wait()
    far_p, far_q = parts(far)
    eight, far_eight = {0: p, 1: q}, {2: far_p, 3: far_q}
    nine = {j: product(m, p) for j, m in eight.items()}
    nine |= {j: product(m, q) for j, m in far_eight.items()}
    far_nine = {j: product(m, far_p) for j, m in far_eight.items()}
    far_nine |= {j: product(m, far_q) for j, m in eight.items()}
    for j in range(4):
        total = times_t(nine[j], p) + times_t(far_nine[j], q)
        total = total + (times(eight[j], k) if j in eight else times(far_eight[j], c))
        out_ref[j] = total.astype(BF16)


def prepare_top_kernel(
    near_ref, eighth_ref, own_ref, maps_ref, links_ref, base_ref, mix_ref, near, eighth, sem
):
    copies = start_copies([(near_ref, near), (eighth_ref, eighth)], sem)
    (p, q), (c, k) = parts(maps_ref), parts(links_ref)
    for copy in copies:
        copy.wait()
    for j in range(4):
        total = times_t(eighth[j], p) + times_t(near[j ^ 1], q)
        if j < 2:
            total = total + (c if j else k).astype(F32)
        matrix = total.astype(BF16)
        if j:
            mix_ref[j - 1] = matrix
        else:
            base_ref[...] = times(own_ref[...], matrix)


def turn(got_shift, product_of, slot_shift, width):
    def kernel(me_ref, got_ref, base_ref, mix_ref, local_ref, maps_ref, own_ref, slots_ref):
        me = me_ref[0]
        total = base_ref[...]
        for k in (1, 2, 3):
            total = total + product_of(got_ref[(me >> got_shift & 3) ^ k], mix_ref[k - 1])
        node = total.astype(BF16)
        own = times_t(node, parts(maps_ref)[0]) + local_ref[...].astype(F32)
        own = own.astype(BF16)
        own_ref[...] = own
        place, half = me >> slot_shift & (1 << width) - 1, 1 << width - 1
        near = place & half
        for k in range(half):
            slots_ref[near | k] = own
            slots_ref[(near ^ half) | k] = node

    return kernel


def prepare_down_kernel(far_ref, own_ref, local_ref, maps_ref, base_ref, mix_ref, far, sem):
    copies = start_copies([(far_ref, far)], sem)
    p, q = parts(maps_ref)
    base_ref[...] = times_t(own_ref[...], p) + local_ref[...].astype(F32)
    mix_ref[0] = q
    mix_ref[1] = product(p, q)
    copies[0].wait()
    mix_ref[2] = product(q, far[...])


def prepare_down_y_kernel(*refs):
    (core_ref, y1_ref, cy_ref, dense_ref, own_ref, one_ref, two_ref, maps_ref, basis_ref) = refs[:9]
    base_ref, mix_ref, core, y1, cy, dense, sem = refs[9:]
    copies = start_copies([(core_ref, core), (y1_ref, y1), (cy_ref, cy), (dense_ref, dense)], sem)
    p, q = parts(maps_ref)
    mix = [product(p, p), None, product(p, q), None]
    for copy in copies:
        copy.wait()
    rank = p.shape[0]
    core_p, core_q, core_two = core[:rank], core[rank : 2 * rank], core[2 * rank :]
    mix[1] = product(q, core_p)
    mix[3] = product(q, core_q)
    node = times_t(own_ref[...], mix[0]) + one_ref[...].astype(F32)
    node = node + times_t(two_ref[...], p) + times_t(core_two, q)
    base_ref[...] = dense[...] + times_t(node.astype(BF16), basis_ref[...])
    for k, far in enumerate((q, core_q, y1[...], cy[...])):
        if k:
            mix_ref[k - 1] = mix[k]
        mix_ref[k + 3] = product(mix[k], far)


def finish_kernel(me_ref, got_ref, base_ref, mix_ref, basis_ref, out_ref):
    me = me_ref[0] & 7
    total = None
    for k in range(1, 8):
        part = times_t(got_ref[me ^ k], mix_ref[k - 1])
        total = part if total is None else total + part
    node = total.astype(BF16)
    out_ref[...] = (base_ref[...] + times_t(node, basis_ref[...])).astype(BF16)


def body(right_sides, leaf_inverse, leaf_basis, transfer, coupling):
    rank = leaf_basis.shape[1]
    columns = right_sides.shape[0]
    block, square = (columns, rank), (rank, rank)
    me = lax.axis_index(AXIS).astype(jnp.int32).reshape(1)
    prefetched, local = {}, {}

    def after(values, late):
        return lax.optimization_barrier((values, late))[0]

    def prefetch(name, value, mask, late):
        value = after(value, late)
        prefetched[name] = swap(value, mask)

    current = times(right_sides, leaf_basis).astype(BF16)
    held = [pltpu.SemaphoreType.DMA((1,))]
    outs = [(transfer.shape, BF16)]
    (transfer,) = call(stage_kernel, outs, [after(transfer, current)], [IN_HBM], held)
    own_map, other_map = transfer[:rank], transfer[rank:]
    from_other, from_own = coupling[:rank], coupling[rank:]

    def settle(level, far, own, late):
        far, own = after((far, own), late)
        total = times(far, from_other) + times(own, from_own)
        local[level] = lax.optimization_barrier(total.astype(BF16))

    late = []

    def half_up(current, bit):
        other = swap(current, 1 << bit)
        part = times(current, own_map)
        return part, other

    def up(current, bit):
        part, other = half_up(current, bit)
        above = (part + times(other, other_map)).astype(BF16)
        late.append((bit + 1, other, current))
        return above

    current = up(current, 0)
    prefetch("pre_z2", transfer, 16, current)
    current = up(current, 1)
    copied = [right_sides, leaf_inverse]
    (dense,) = call(
        dense_kernel,
        [((columns, leaf_inverse.shape[1]), F32)],
        [after(right_sides, current), leaf_inverse],
        [IN_HBM] * 2,
        [pltpu.VMEM(a.shape, a.dtype) for a in copied] + [pltpu.SemaphoreType.DMA((CHUNKS + 1,))],
        None,
    )
    below = current
    part, other = half_up(below, 2)

    current, slots = call(
        open_up_z_kernel,
        [(block, BF16), ((4, *block), BF16)],
        [me, part, other, transfer],
        [IN_SMEM] + [IN_VMEM] * 3,
    )
    late.append((3, other, below))
    prefetch("pre_x2", transfer, 256, slots)
    got = exchange(slots, 3, 2)
    far = prefetched["pre_z2"]
    base, mix = call(
        prepare_up_z_kernel,
        [(block, F32), ((3, *square), BF16)],
        [far, current, transfer],
        [IN_HBM] + [IN_VMEM] * 2,
        fetched([far]),
    )
    below = current
    (current,) = call(
        close_up_z_kernel, [(block, BF16)], [me, got, base, mix], [IN_SMEM] + [IN_VMEM] * 3
    )
    (settled,) = call(
        settle_up_z_kernel,
        [((2, *block), BF16)],
        [me, got, after(below, current), far, transfer, coupling],
        [IN_SMEM, IN_VMEM, IN_VMEM, IN_HBM, IN_VMEM, IN_VMEM],
        fetched([far]),
    )
    far = prefetched["pre_x2"]
    (eighth,) = call(
        eighth_kernel,
        [((4, *square), BF16)],
        [far, after(transfer, current), coupling],
        [IN_HBM, IN_VMEM, IN_VMEM],
        fetched([far]),
    )
    for level, far_t, own_t in late:
        settle(level, far_t, own_t, current)
    late.clear()
    current = up(current, 5)
    prefetch("pre_x1", eighth, 128, current)
    prefetch("pre_q_z4", after(transfer, current)[rank:], 32, current)
    below = current
    part, other = half_up(below, 6)

    current, slots = call(
        open_top_kernel,
        [(block, BF16), ((4, *block), BF16)],
        [part, other, transfer],
        [IN_VMEM] * 3,
    )
    settle(7, other, below, current)
    for level, far_t, own_t in late:
        settle(level, far_t, own_t, slots)
    got = exchange(slots, 7, 2)
    near = prefetched["pre_x1"]
    base, mix = call(
        prepare_top_kernel,
        [(block, F32), ((3, *square), BF16)],
        [near, eighth, current, transfer, coupling],
        [IN_HBM] * 2 + [IN_VMEM] * 3,
        fetched([near, eighth]),
    )
    local[4], local[5] = settled[0], settled[1]

    def turn_down(kernel, got, base, mix, level, width):
        return call(
            kernel,
            [(block, BF16), ((1 << width, *block), BF16)],
            [me, got, base, mix, local[level], transfer],
            [IN_SMEM] + [IN_VMEM] * 5,
        )

    def prepare_down(far, own, level):
        return call(
            prepare_down_kernel,
            [(block, F32), ((3, *square), BF16)],
            [far, own, local[level], transfer],
            [IN_HBM] + [IN_VMEM] * 3,
            fetched([far]),
        )

    own, slots = turn_down(turn(7, times, 5, 2), got, base, mix, 7, 2)
    neighbour_map = after(transfer, slots)[rank:]
    prefetch("pre_q_y1", neighbour_map, 2, slots)
    prefetch("pre_q_cy", neighbour_map, 3, slots)
    prefetch("pre_q_z1", neighbour_map, 8, slots)
    got = exchange(slots, 5, 2)
    base, mix = prepare_down(prefetched["pre_q_z4"], own, 6)

    own, slots = turn_down(turn(5, times_t, 3, 2), got, base, mix, 5, 2)
    prefetch("pre_core", jnp.concatenate(after((transfer, local[2]), slots), 0), 1, slots)
    got = exchange(slots, 3, 2)
    base, mix = prepare_down(prefetched["pre_q_z1"], own, 4)

    own, slots = turn_down(turn(3, times_t, 0, 3), got, base, mix, 3, 3)
    got = exchange(slots, 0, 3)
    near = [prefetched[f"pre_{name}"] for name in ("core", "q_y1", "q_cy")]
    base, mix = call(
        prepare_down_y_kernel,
        [(dense.shape, F32), ((7, *square), BF16)],
        [*near, dense, own, local[1], local[2], transfer, leaf_basis],
        [IN_HBM] * 4 + [IN_VMEM] * 5,
        fetched([*near, dense]),
    )
    (out,) = call(
        finish_kernel,
        [(dense.shape, BF16)],
        [me, got, base, mix, leaf_basis],
        [IN_SMEM] + [IN_VMEM] * 4,
    )
    return out


def solution(mesh):
    placed = (P(None, AXIS), P(AXIS, None), P(AXIS, None), P(AXIS, None), P(AXIS, None))
    return jax.shard_map(
        body, mesh=mesh, in_specs=placed, out_specs=P(None, AXIS), check_vma=False
    )
```

```python
import jax
import jax.numpy as jnp
from jax import lax
from jax.experimental import pallas as pl
from jax.experimental.pallas import tpu as pltpu
from jax.sharding import PartitionSpec as P


AXIS = "leaf"
BF16 = jnp.bfloat16
F32 = jnp.float32
CHUNKS = 4
VMEM_GRANT = 12 * 2**20


IN_SMEM = pl.BlockSpec(memory_space=pltpu.SMEM)
IN_VMEM = pl.BlockSpec(memory_space=pltpu.VMEM)
IN_HBM = pl.BlockSpec(memory_space=pltpu.HBM)


def swap(block, mask):
    route = [(device, device ^ mask) for device in range(lax.axis_size(AXIS))]
    return lax.ppermute(block, AXIS, route)


def exchange(slots, low, width):
    count, size = lax.axis_size(AXIS), 1 << width
    groups = [
        [base | k << low for k in range(size)]
        for base in range(count)
        if not base & ((size - 1) << low)
    ]
    return lax.all_to_all(slots, AXIS, 0, 0, axis_index_groups=groups)


def times(values, matrix):
    return jnp.dot(values, matrix, preferred_element_type=F32)


def times_t(values, matrix):
    return lax.dot_general(values, matrix, (((1,), (1,)), ((), ())), preferred_element_type=F32)


def product(*matrices):
    total = matrices[0]
    for matrix in matrices[1:]:
        total = times(total, matrix).astype(BF16)
    return total


def call(kernel, outs, ins, specs, scratch=(), grant=VMEM_GRANT, out_specs=None):
    outs = [jax.ShapeDtypeStruct(shape, dtype) for shape, dtype in outs]
    return pl.pallas_call(
        kernel,
        out_shape=outs,
        in_specs=specs,
        out_specs=out_specs or [IN_VMEM] * len(outs),
        scratch_shapes=list(scratch),
        compiler_params=pltpu.CompilerParams(vmem_limit_bytes=grant),
    )(*ins)


def fetched(arrays):
    return [pltpu.VMEM(a.shape, a.dtype) for a in arrays] + [pltpu.SemaphoreType.DMA((len(arrays),))]


def start_copies(pairs, arrived):
    copies = [
        pltpu.make_async_copy(source, target, arrived.at[k])
        for k, (source, target) in enumerate(pairs)
    ]
    for copy in copies:
        copy.start()
    return copies


def stage_kernel(source_ref, out_ref, sem):
    start_copies([(source_ref, out_ref)], sem)[0].wait()


def dense_kernel(sides_ref, inverse_ref, out_ref, sides, inverse, sem):
    rows = inverse.shape[0] // CHUNKS
    cuts = [pl.ds(k * rows, rows) for k in range(CHUNKS)]
    copies = start_copies(
        [(sides_ref, sides)] + [(inverse_ref.at[cut], inverse.at[cut]) for cut in cuts], sem
    )
    copies[0].wait()
    total = None
    for k in range(CHUNKS):
        copies[k + 1].wait()
        cut = slice(k * rows, (k + 1) * rows)
        part = times(sides[:, cut], inverse[cut])
        total = part if total is None else total + part
    out_ref[...] = total


def parts(maps_ref):
    rank = maps_ref.shape[1]
    return [maps_ref[k * rank : (k + 1) * rank] for k in range(maps_ref.shape[0] // rank)]


def open_up_z_kernel(me_ref, part_ref, other_ref, maps_ref, own_ref, slots_ref):
    p, q = parts(maps_ref)
    own = (part_ref[...] + times(other_ref[...], q)).astype(BF16)
    own_ref[...] = own
    for k in range(4):
        slots_ref[k] = own
    slots_ref[(me_ref[0] >> 3 & 3) ^ 2] = times(own, p).astype(BF16)


def prepare_up_z_kernel(far_ref, own_ref, maps_ref, base_ref, mix_ref, far, sem):
    copies = start_copies([(far_ref, far)], sem)
    p, q = parts(maps_ref)
    base_ref[...] = times(own_ref[...], product(p, p))
    mix_ref[0] = product(q, p)
    mix_ref[1] = q
    copies[0].wait()
    mix_ref[2] = product(parts(far)[1], q)


def close_up_z_kernel(me_ref, got_ref, base_ref, mix_ref, out_ref):
    me = me_ref[0] >> 3 & 3
    total = base_ref[...]
    for k in (1, 2, 3):
        total = total + times(got_ref[me ^ k], mix_ref[k - 1])
    out_ref[...] = total.astype(BF16)


def settle_up_z_kernel(me_ref, got_ref, own_ref, far_ref, maps_ref, links_ref, out_ref, far, sem):
    copies = start_copies([(far_ref, far)], sem)
    me = me_ref[0] >> 3 & 3
    (p, q), (c, k) = parts(maps_ref), parts(links_ref)
    own, near = own_ref[...], got_ref[me ^ 1]
    out_ref[0] = (times(near, c) + times(own, k)).astype(BF16)
    middle = (times(own, p) + times(near, q)).astype(BF16)
    copies[0].wait()
    across = (got_ref[me ^ 2].astype(F32) + times(got_ref[me ^ 3], parts(far)[1])).astype(BF16)
    out_ref[1] = (times(across, c) + times(middle, k)).astype(BF16)


def open_top_kernel(part_ref, other_ref, maps_ref, own_ref, slots_ref):
    own = (part_ref[...] + times(other_ref[...], parts(maps_ref)[1])).astype(BF16)
    own_ref[...] = own
    for k in range(4):
        slots_ref[k] = own


def eighth_kernel(far_ref, maps_ref, links_ref, out_ref, far, sem):
    copies = start_copies([(far_ref, far)], sem)
    (p, q), (c, k) = parts(maps_ref), parts(links_ref)
    copies[0].wait()
    far_p, far_q = parts(far)
    eight, far_eight = {0: p, 1: q}, {2: far_p, 3: far_q}
    nine = {j: product(m, p) for j, m in eight.items()}
    nine |= {j: product(m, q) for j, m in far_eight.items()}
    far_nine = {j: product(m, far_p) for j, m in far_eight.items()}
    far_nine |= {j: product(m, far_q) for j, m in eight.items()}
    for j in range(4):
        total = times_t(nine[j], p) + times_t(far_nine[j], q)
        total = total + (times(eight[j], k) if j in eight else times(far_eight[j], c))
        out_ref[j] = total.astype(BF16)


def prepare_top_kernel(
    near_ref, eighth_ref, own_ref, maps_ref, links_ref, base_ref, mix_ref, near, eighth, sem
):
    copies = start_copies([(near_ref, near), (eighth_ref, eighth)], sem)
    (p, q), (c, k) = parts(maps_ref), parts(links_ref)
    for copy in copies:
        copy.wait()
    for j in range(4):
        total = times_t(eighth[j], p) + times_t(near[j ^ 1], q)
        if j < 2:
            total = total + (c if j else k).astype(F32)
        matrix = total.astype(BF16)
        if j:
            mix_ref[j - 1] = matrix
        else:
            base_ref[...] = times(own_ref[...], matrix)


def turn(got_shift, product_of, slot_shift, width):
    def kernel(me_ref, got_ref, base_ref, mix_ref, local_ref, maps_ref, own_ref, slots_ref, held, sem):
        me = me_ref[0]
        total = base_ref[...]
        for k in (1, 2, 3):
            total = total + product_of(got_ref[(me >> got_shift & 3) ^ k], mix_ref[k - 1])
        node = total.astype(BF16)
        held[...] = node
        place, half = me >> slot_shift & (1 << width) - 1, 1 << width - 1
        near = place & half
        far = [
            pltpu.make_async_copy(held, slots_ref.at[(near ^ half) | k], sem.at[k])
            for k in range(half)
        ]
        for copy in far:
            copy.start()
        own = times_t(node, parts(maps_ref)[0]) + local_ref[...].astype(F32)
        own_ref[...] = own.astype(BF16)
        beside = [
            pltpu.make_async_copy(own_ref, slots_ref.at[near | k], sem.at[half + k])
            for k in range(half)
        ]
        for copy in beside:
            copy.start()
        for copy in far + beside:
            copy.wait()

    return kernel


def prepare_down_kernel(far_ref, own_ref, local_ref, maps_ref, base_ref, mix_ref, far, sem):
    copies = start_copies([(far_ref, far)], sem)
    p, q = parts(maps_ref)
    base_ref[...] = times_t(own_ref[...], p) + local_ref[...].astype(F32)
    mix_ref[0] = q
    mix_ref[1] = product(p, q)
    copies[0].wait()
    mix_ref[2] = product(q, far[...])


def prepare_down_y_kernel(*refs):
    (core_ref, y1_ref, cy_ref, dense_ref, own_ref, one_ref, two_ref, maps_ref, basis_ref) = refs[:9]
    base_ref, mix_ref, core, y1, cy, dense, sem = refs[9:]
    copies = start_copies([(core_ref, core), (y1_ref, y1), (cy_ref, cy), (dense_ref, dense)], sem)
    p, q = parts(maps_ref)
    mix = [product(p, p), None, product(p, q), None]
    for copy in copies:
        copy.wait()
    rank = p.shape[0]
    core_p, core_q, core_two = core[:rank], core[rank : 2 * rank], core[2 * rank :]
    mix[1] = product(q, core_p)
    mix[3] = product(q, core_q)
    node = times_t(own_ref[...], mix[0]) + one_ref[...].astype(F32)
    node = node + times_t(two_ref[...], p) + times_t(core_two, q)
    base_ref[...] = dense[...] + times_t(node.astype(BF16), basis_ref[...])
    for k, far in enumerate((q, core_q, y1[...], cy[...])):
        if k:
            mix_ref[k - 1] = mix[k]
        mix_ref[k + 3] = product(mix[k], far)


def finish_kernel(me_ref, got_ref, base_ref, mix_ref, basis_ref, out_ref):
    me = me_ref[0] & 7
    total = None
    for k in range(1, 8):
        part = times_t(got_ref[me ^ k], mix_ref[k - 1])
        total = part if total is None else total + part
    node = total.astype(BF16)
    out_ref[...] = (base_ref[...] + times_t(node, basis_ref[...])).astype(BF16)


def body(right_sides, leaf_inverse, leaf_basis, transfer, coupling):
    rank = leaf_basis.shape[1]
    columns = right_sides.shape[0]
    block, square = (columns, rank), (rank, rank)
    me = lax.axis_index(AXIS).astype(jnp.int32).reshape(1)
    prefetched, local = {}, {}

    def after(values, late):
        return lax.optimization_barrier((values, late))[0]

    def prefetch(name, value, mask, late):
        value = after(value, late)
        prefetched[name] = swap(value, mask)

    current = times(right_sides, leaf_basis).astype(BF16)
    held = [pltpu.SemaphoreType.DMA((1,))]
    outs = [(transfer.shape, BF16)]
    (transfer,) = call(stage_kernel, outs, [after(transfer, current)], [IN_HBM], held)
    own_map, other_map = transfer[:rank], transfer[rank:]
    from_other, from_own = coupling[:rank], coupling[rank:]

    def settle(level, far, own, late):
        far, own = after((far, own), late)
        total = times(far, from_other) + times(own, from_own)
        local[level] = lax.optimization_barrier(total.astype(BF16))

    late = []

    def half_up(current, bit):
        other = swap(current, 1 << bit)
        part = times(current, own_map)
        return part, other

    def up(current, bit):
        part, other = half_up(current, bit)
        above = (part + times(other, other_map)).astype(BF16)
        late.append((bit + 1, other, current))
        return above

    current = up(current, 0)
    prefetch("pre_z2", transfer, 16, current)
    current = up(current, 1)
    copied = [right_sides, leaf_inverse]
    (dense,) = call(
        dense_kernel,
        [((columns, leaf_inverse.shape[1]), F32)],
        [after(right_sides, current), leaf_inverse],
        [IN_HBM] * 2,
        [pltpu.VMEM(a.shape, a.dtype) for a in copied] + [pltpu.SemaphoreType.DMA((CHUNKS + 1,))],
        None,
    )
    below = current
    part, other = half_up(below, 2)

    current, slots = call(
        open_up_z_kernel,
        [(block, BF16), ((4, *block), BF16)],
        [me, part, other, transfer],
        [IN_SMEM] + [IN_VMEM] * 3,
    )
    late.append((3, other, below))
    prefetch("pre_x2", transfer, 256, slots)
    got = exchange(slots, 3, 2)
    far = prefetched["pre_z2"]
    base, mix = call(
        prepare_up_z_kernel,
        [(block, F32), ((3, *square), BF16)],
        [far, current, transfer],
        [IN_HBM] + [IN_VMEM] * 2,
        fetched([far]),
    )
    below = current
    (current,) = call(
        close_up_z_kernel, [(block, BF16)], [me, got, base, mix], [IN_SMEM] + [IN_VMEM] * 3
    )
    (settled,) = call(
        settle_up_z_kernel,
        [((2, *block), BF16)],
        [me, got, after(below, current), far, transfer, coupling],
        [IN_SMEM, IN_VMEM, IN_VMEM, IN_HBM, IN_VMEM, IN_VMEM],
        fetched([far]),
    )
    far = prefetched["pre_x2"]
    (eighth,) = call(
        eighth_kernel,
        [((4, *square), BF16)],
        [far, after(transfer, current), coupling],
        [IN_HBM, IN_VMEM, IN_VMEM],
        fetched([far]),
    )
    for level, far_t, own_t in late:
        settle(level, far_t, own_t, current)
    late.clear()
    current = up(current, 5)
    prefetch("pre_x1", eighth, 128, current)
    prefetch("pre_q_z4", after(transfer, current)[rank:], 32, current)
    below = current
    part, other = half_up(below, 6)

    current, slots = call(
        open_top_kernel,
        [(block, BF16), ((4, *block), BF16)],
        [part, other, transfer],
        [IN_VMEM] * 3,
    )
    settle(7, other, below, current)
    for level, far_t, own_t in late:
        settle(level, far_t, own_t, slots)
    got = exchange(slots, 7, 2)
    near = prefetched["pre_x1"]
    base, mix = call(
        prepare_top_kernel,
        [(block, F32), ((3, *square), BF16)],
        [near, eighth, current, transfer, coupling],
        [IN_HBM] * 2 + [IN_VMEM] * 3,
        fetched([near, eighth]),
    )
    local[4], local[5] = settled[0], settled[1]

    def turn_down(kernel, got, base, mix, level, width):
        return call(
            kernel,
            [(block, BF16), ((1 << width, *block), BF16)],
            [me, got, base, mix, local[level], transfer],
            [IN_SMEM] + [IN_VMEM] * 5,
            [pltpu.VMEM(block, BF16), pltpu.SemaphoreType.DMA((1 << width,))],
            out_specs=[IN_VMEM, IN_HBM],
        )

    def prepare_down(far, own, level):
        return call(
            prepare_down_kernel,
            [(block, F32), ((3, *square), BF16)],
            [far, own, local[level], transfer],
            [IN_HBM] + [IN_VMEM] * 3,
            fetched([far]),
        )

    own, slots = turn_down(turn(7, times, 5, 2), got, base, mix, 7, 2)
    neighbour_map = after(transfer, slots)[rank:]
    prefetch("pre_q_y1", neighbour_map, 2, slots)
    prefetch("pre_q_cy", neighbour_map, 3, slots)
    prefetch("pre_q_z1", neighbour_map, 8, slots)
    got = exchange(slots, 5, 2)
    base, mix = prepare_down(prefetched["pre_q_z4"], own, 6)

    own, slots = turn_down(turn(5, times_t, 3, 2), got, base, mix, 5, 2)
    prefetch("pre_core", jnp.concatenate(after((transfer, local[2]), slots), 0), 1, slots)
    got = exchange(slots, 3, 2)
    base, mix = prepare_down(prefetched["pre_q_z1"], own, 4)

    own, slots = turn_down(turn(3, times_t, 0, 3), got, base, mix, 3, 3)
    got = exchange(slots, 0, 3)
    near = [prefetched[f"pre_{name}"] for name in ("core", "q_y1", "q_cy")]
    base, mix = call(
        prepare_down_y_kernel,
        [(dense.shape, F32), ((7, *square), BF16)],
        [*near, dense, own, local[1], local[2], transfer, leaf_basis],
        [IN_HBM] * 4 + [IN_VMEM] * 5,
        fetched([*near, dense]),
    )
    (out,) = call(
        finish_kernel,
        [(dense.shape, BF16)],
        [me, got, base, mix, leaf_basis],
        [IN_SMEM] + [IN_VMEM] * 4,
    )
    return out


def solution(mesh):
    placed = (P(None, AXIS), P(AXIS, None), P(AXIS, None), P(AXIS, None), P(AXIS, None))
    return jax.shard_map(
        body, mesh=mesh, in_specs=placed, out_specs=P(None, AXIS), check_vma=False
    )
```
